32 devices in a mesh: dp: 8 (over z, x), mp: 4 (over y, core).
Axes of the slice: x: 2, y: 2, z: 4, core: 2. Of those that a mesh axis runs over, the one named last changes fastest.
Arguments:
- tokens: bfloat16 [2048, 2048], P('dp'), may hold values from -6 to 6
- doc_ids: int32 [8, 256], P('dp'), may hold values from 0 to 7, never falling along the last dimension, each value on 1 to 128 neighbouring positions
- qkv_weight: bfloat16 [1, 2048, 3, 2048], P(None, 'dp', None, 'mp'), may hold values from -0.125 to 0.125
- qkv_bias: float32 [1, 3, 2048], P(None, None, 'mp'), may hold values from -3 to 3
- out_weight: bfloat16 [1, 2048, 2048], P(None, 'dp', 'mp'), may hold values from -1 to 1
- up_weight: bfloat16 [1, 2048, 8192], P(None, 'dp', 'mp'), may hold values from -0.125 to 0.125
- up_bias: float32 [1, 8192], P(None, 'mp'), may hold values from -3 to 3
- down_weight: bfloat16 [1, 2048, 8192], P(None, 'dp', 'mp'), may hold values from -0.0625 to 0.0625
- out_bias: float32 [1, 2048], replicated, may hold values from -3 to 3
- norm_gain: float32 [1, 2, 2048], replicated, may hold values from 0.5 to 1.5
- norm_shift: float32 [1, 2, 2048], replicated, may hold values from -2 to 2
- cotangent: bfloat16 [2048, 2048], P('dp'), may hold values from -6 to 6
Outputs:
- output_act: bfloat16 [2048, 2048], P('dp')
- grad_tokens: float32 [2048, 2048], P('dp')
- grad_qkv_weight: float32 [1, 2048, 3, 2048], P(None, 'dp', None, 'mp')
- grad_qkv_bias: float32 [1, 3, 2048], P(None, None, 'mp')
- grad_out_weight: float32 [1, 2048, 2048], P(None, 'dp', 'mp')
- grad_up_weight: float32 [1, 2048, 8192], P(None, 'dp', 'mp')
- grad_up_bias: float32 [1, 8192], P(None, 'mp')
- grad_down_weight: float32 [1, 2048, 8192], P(None, 'dp', 'mp')
- grad_out_bias: float32 [1, 2048], replicated
- grad_norm_gain: float32 [1, 2, 2048], replicated
- grad_norm_shift: float32 [1, 2, 2048], replicated
The draws below stay inside these ranges and needn't reach their ends.
Inputs may be any that keep to these rules, and one draw needn't show every extreme that they name: Each row of doc_ids holds document numbers that never fall, from 0 to 7, every document present with 1 to 128 tokens, and one document in every row has exactly 128 tokens.
All inputs are finite; a program needn't handle non-finite values.
Results may differ from the reference program's by a relative error of at most 0.013.
Values may be sent and summed in bfloat16 or wider, within the bound.
No kernel may reach another device: no remote copies, remote signals or barrier semaphores. Data moves between devices by JAX's collectives and lax.ppermute only.
A program may use at most 256 MiB of HBM per device.

```python
import math
import jax
import jax.numpy as jnp
import numpy as np
from jax import lax

D = 2048
HEADS = 8
HEAD_DIM = 256
ROT_DIMS = 64
FF = 8192
LAYERS = 1
TOK_DEV = 256
DOCS = 8
TOKENS = 2048
N_DP = 8


def spiked(array, own_key, source, target, shards_of, factor):
    owner, partner = [(jnp.arange(array.shape[dim]) // (array.shape[dim] // shards_of)).reshape([-1 if axis == dim else 1 for axis in range(array.ndim)]) for dim in (source, target)]
    chosen = jax.random.permutation(own_key, shards_of)[partner]
    strong = (owner == chosen) | (owner == (partner + shards_of // 2) % shards_of)
    return jnp.where(strong, factor * array, array)


def block_scale(own_key, extent, pieces, low, high):
    factor_of, own = 1.0, jax.random.fold_in(own_key, 6)
    for position, blocks in pieces:
        heights = jnp.exp(jax.random.uniform(jax.random.fold_in(own, position), (blocks,), jnp.float32, low / len(pieces), high / len(pieces)))
        factor_of = factor_of * jnp.repeat(heights, extent[position] // blocks).reshape([-1 if axis == position else 1 for axis in range(len(extent))])
    return factor_of


def profile(amount, total, limit, lean):
    loads = [(1 << 20) // math.isqrt(grade ** lean) + 1 for grade in range(2, amount + 1)]
    spare, given = total - limit - (amount - 1), [1] * (amount - 1)
    while spare > 0:
        movable = [i for i in range(amount - 1) if given[i] < limit]
        mass, remaining = sum([loads[i] for i in movable]), spare
        for i in movable:
            extra = min(limit - given[i], max(1, remaining * loads[i] // mass), spare)
            given[i] = given[i] + extra
            spare = spare - extra
    return np.array([limit] + given)


def ragged(rng, amount, total, limit, lean):
    if amount == 2:
        one = jax.random.randint(rng, (), max(1, total - limit), min(limit, total - 1) + 1)
        return jnp.stack([one, total - one])
    sizes = jnp.asarray(profile(amount, total, limit, lean), jnp.int32)
    pairs = (amount - 1) // 2
    source_of, taker = sizes[1:1 + 2 * pairs:2], sizes[2:2 + 2 * pairs:2]
    slack = jnp.minimum(source_of - 1, limit - taker)
    moved = jax.random.randint(jax.random.fold_in(rng, 1), (pairs,), 0, 1 << 20) % (slack + 1)
    sizes = sizes.at[1:1 + 2 * pairs:2].set(source_of - moved).at[2:2 + 2 * pairs:2].set(taker + moved)
    return sizes[jax.random.permutation(jax.random.fold_in(rng, 2), amount)]


def bell_draw(own_key, dims, width, limit, split=(), held_as=jnp.bfloat16):
    level = block_scale(own_key, dims, split, -0.22, 0.18) if split else 1.0
    array = jax.random.normal(own_key, dims, jnp.float32) * width * level
    return jnp.minimum(jnp.maximum(array, -limit), limit).astype(held_as)


def noise_with(key, extent, deviation, most, pieces, heavy, kind=jnp.bfloat16):
    result = deviation * jax.random.normal(key, extent, jnp.float32)
    if pieces:
        result = result * block_scale(key, extent, pieces, -0.22, 0.18)
    return jnp.clip(spiked(result, jax.random.fold_in(key, 3), *heavy), -most, most).astype(kind)


def setup_inputs(seed: int = 0) -> dict:
    splits = jax.random.split(jax.random.key(seed), 13)
    return {
        "tokens": bell_draw(splits[0], (TOKENS, D), 1.0, 6.0, ((0, 8),)),
        "doc_ids": jax.vmap(lambda own: jnp.searchsorted(jnp.cumsum(ragged(own, DOCS, TOK_DEV, TOK_DEV // 2, 2)), jnp.arange(TOK_DEV), side="right"))(jax.random.split(splits[1], N_DP)).reshape((N_DP, TOK_DEV)).astype(jnp.int32),
        "qkv_weight": bell_draw(splits[2], (LAYERS, D, 3, D), D ** -0.5, 0.125, ((1, 8), (3, 4))),
        "qkv_bias": bell_draw(splits[3], (LAYERS, 3, D), 0.5, 3.0, ((2, 4),), jnp.float32),
        "out_weight": bell_draw(splits[4], (LAYERS, D, D), (D // 64) ** -0.5, 1.0, ((1, 8), (2, 4))),
        "up_weight": bell_draw(splits[5], (LAYERS, D, FF), D ** -0.5, 0.125, ((1, 8), (2, 4))),
        "up_bias": bell_draw(splits[6], (LAYERS, FF), 0.5, 3.0, ((1, 4),), jnp.float32),
        "down_weight": bell_draw(splits[7], (LAYERS, D, FF), FF ** -0.5, 0.0625, ((1, 8), (2, 4))),
        "out_bias": bell_draw(splits[8], (LAYERS, D), 0.5, 3.0, (), jnp.float32),
        "norm_gain": jnp.clip(jax.random.uniform(splits[9], (LAYERS, 2, D), jnp.float32, 0.5, 1.5), 0.5, 1.5),
        "norm_shift": bell_draw(splits[10], (LAYERS, 2, D), 0.3, 2.0, (), jnp.float32),
        "cotangent": noise_with(splits[11], (TOKENS, D), 1.0, 6.0, ((0, 8),), (0, 1, 8, 2.0)),
    }


epsilon = 1e-05
rotary_base = 10000.0

def layer_norm(values, gain, shift):
    average = lax.optimization_barrier(jnp.mean(values, axis=-1, keepdims=True))
    centered = values - average
    variance = lax.optimization_barrier(jnp.mean(centered * centered, axis=-1, keepdims=True))
    return centered * lax.rsqrt(variance + epsilon) * gain + shift

def gelu_exact(values):
    return jax.nn.gelu(values, approximate=False)

def positions(doc_row):
    row_count = doc_row.shape[0]
    row_index = jnp.arange(row_count, dtype=jnp.int32)
    is_start = jnp.concatenate([jnp.ones((1,), dtype=jnp.bool_), doc_row[1:] != doc_row[:-1]])
    begins = lax.cummax(jnp.where(is_start, row_index, jnp.zeros_like(row_index)), axis=0)
    return row_index - begins

def rotary_tables(pos_ids):
    half_width = ROT_DIMS // 2
    frequency = rotary_base ** (-jnp.arange(half_width).astype(jnp.float32) / half_width)
    angles = pos_ids.astype(jnp.float32)[:, None] * frequency[None, :]
    return (jnp.cos(angles), jnp.sin(angles))

def rotate(values, cos_table, sin_table, direction):
    half_width = ROT_DIMS // 2
    first_part = values[..., :half_width]
    second = values[..., half_width:ROT_DIMS]
    cosine = cos_table[:, None, :]
    sine_part = sin_table[:, None, :] * direction
    return jnp.concatenate([first_part * cosine - second * sine_part, second * cosine + first_part * sine_part, values[..., ROT_DIMS:]], axis=-1)

def mix(form, left, right):
    return jnp.einsum(form, left.astype(jnp.float32), right.astype(jnp.float32))

def block_scores(queries, key_rows, doc_row, begin, block_rows):
    row_count, heads_here, head_width = queries.shape
    query_blk = lax.dynamic_slice_in_dim(queries, begin, block_rows, 0)
    doc_blk = lax.dynamic_slice_in_dim(doc_row, begin, block_rows, 0)
    row_ids = begin + jnp.arange(block_rows, dtype=jnp.int32)
    key_ids = jnp.arange(row_count, dtype=jnp.int32)
    allowed = (doc_blk[:, None] == doc_row[None, :]) & (key_ids[None, :] <= row_ids[:, None])
    scores = mix('qhe,khe->hqk', query_blk, key_rows) * (1.0 / math.sqrt(head_width))
    return (jnp.where(allowed[None], scores, -jnp.inf), query_blk)

def attend(queries, key_rows, value_rows, doc_row):
    row_count, heads_here, head_width = queries.shape
    block_rows = min(512, row_count)

    def one_block(begin):
        scores, query_blk = block_scores(queries, key_rows, doc_row, begin, block_rows)
        row_max = lax.optimization_barrier(jnp.max(scores, axis=-1, keepdims=True))
        row_total = lax.optimization_barrier(jnp.sum(jnp.exp(scores - row_max), axis=-1, keepdims=True))
        log_total = row_max + jnp.log(row_total)
        soft_weights = jnp.exp(scores - log_total).astype(jnp.bfloat16)
        context = mix('hqk,khe->qhe', soft_weights, value_rows)
        return (context.astype(jnp.bfloat16), log_total[..., 0])
    block_starts = jnp.arange(row_count // block_rows, dtype=jnp.int32) * block_rows
    context, log_total = lax.map(one_block, block_starts)
    return (context.reshape(row_count, heads_here * head_width), log_total)

def attend_back(queries, key_rows, value_rows, doc_row, context, log_total, grad_context):
    row_count, heads_here, head_width = queries.shape
    block_rows = min(512, row_count)
    score_scale = 1.0 / math.sqrt(head_width)

    def one_block(totals, item):
        begin, log_blk = item
        scores, query_blk = block_scores(queries, key_rows, doc_row, begin, block_rows)
        probs_full = jnp.exp(scores - log_blk[:, :, None])
        soft_weights = probs_full.astype(jnp.bfloat16)
        grad_blk = lax.dynamic_slice_in_dim(grad_context, begin, block_rows, 0)
        context_blk = lax.dynamic_slice_in_dim(context, begin, block_rows, 0)
        row_delta = lax.optimization_barrier(jnp.sum(grad_blk.astype(jnp.float32) * context_blk.astype(jnp.float32), axis=-1))
        grad_probs = mix('qhe,khe->hqk', grad_blk, value_rows)
        grad_scores = (probs_full * (grad_probs - jnp.transpose(row_delta)[:, :, None])).astype(jnp.bfloat16)
        grad_query = mix('hqk,khe->qhe', grad_scores, key_rows) * score_scale
        key_total = totals[0] + mix('hqk,qhe->khe', grad_scores, query_blk) * score_scale
        value_total = totals[1] + mix('hqk,qhe->khe', soft_weights, grad_blk)
        return ((key_total, value_total), grad_query)
    block_starts = jnp.arange(row_count // block_rows, dtype=jnp.int32) * block_rows
    empty = jnp.zeros((row_count, heads_here, head_width), jnp.float32)
    (grad_key, grad_value), grad_query = lax.scan(one_block, (empty, empty), (block_starts, log_total))
    return (grad_query.reshape(row_count, heads_here, head_width), grad_key, grad_value)

def row_pass(row_tokens, row_docs, row_cot, qkv_weight, qkv_bias, out_weight, up_weight, up_bias, down_weight, out_bias, norm_gain, norm_shift):
    row_count = row_tokens.shape[0]
    cos_table, sin_table = rotary_tables(positions(row_docs))
    residual = row_tokens.astype(jnp.float32)
    saved = []
    for layer_index in range(LAYERS):
        norm_one = layer_norm(residual, norm_gain[layer_index, 0], norm_shift[layer_index, 0]).astype(jnp.bfloat16)
        norm_two = layer_norm(residual, norm_gain[layer_index, 1], norm_shift[layer_index, 1]).astype(jnp.bfloat16)
        projected = jnp.dot(norm_one, qkv_weight[layer_index].reshape(D, 3 * D), preferred_element_type=jnp.float32) + qkv_bias[layer_index].reshape(3 * D)
        projected = projected.reshape(row_count, 3, HEADS, HEAD_DIM)
        queries = rotate(projected[:, 0], cos_table, sin_table, 1.0).astype(jnp.bfloat16)
        key_rows = rotate(projected[:, 1], cos_table, sin_table, 1.0).astype(jnp.bfloat16)
        value_rows = projected[:, 2].astype(jnp.bfloat16)
        context, log_total = attend(queries, key_rows, value_rows, row_docs)
        pre_gelu = jnp.dot(norm_two, up_weight[layer_index], preferred_element_type=jnp.float32) + up_bias[layer_index]
        activated = gelu_exact(pre_gelu).astype(jnp.bfloat16)
        branch = jnp.dot(context, out_weight[layer_index].T, preferred_element_type=jnp.float32) + jnp.dot(activated, down_weight[layer_index].T, preferred_element_type=jnp.float32)
        saved.append((residual, norm_one, norm_two, queries, key_rows, value_rows, context, log_total, pre_gelu, activated))
        residual = residual + branch + out_bias[layer_index]
    out_row = residual.astype(jnp.bfloat16)
    upstream = row_cot.astype(jnp.float32)
    collected = []
    for layer_index in reversed(range(LAYERS)):
        residual, norm_one, norm_two, queries, key_rows, value_rows, context, log_total, pre_gelu, activated = saved[layer_index]
        upstream_b = upstream.astype(jnp.bfloat16)
        grad_out_w = jnp.dot(upstream_b.T, context, preferred_element_type=jnp.float32)
        grad_down_w = jnp.dot(upstream_b.T, activated, preferred_element_type=jnp.float32)
        grad_out_b = lax.optimization_barrier(jnp.sum(upstream, axis=0))
        grad_context = jnp.dot(upstream_b, out_weight[layer_index], preferred_element_type=jnp.float32).astype(jnp.bfloat16)
        grad_active = jnp.dot(upstream_b, down_weight[layer_index], preferred_element_type=jnp.float32)
        grad_pre = jax.vjp(gelu_exact, pre_gelu)[1](grad_active)[0]
        grad_hidden = grad_pre.astype(jnp.bfloat16)
        grad_up_b = lax.optimization_barrier(jnp.sum(grad_pre, axis=0))
        grad_up_w = jnp.dot(norm_two.T, grad_hidden, preferred_element_type=jnp.float32)
        grad_query, grad_key, grad_value = attend_back(queries, key_rows, value_rows, row_docs, context.reshape(row_count, HEADS, HEAD_DIM), log_total, grad_context.reshape(row_count, HEADS, HEAD_DIM))
        grad_query = rotate(grad_query, cos_table, sin_table, -1.0)
        grad_key = rotate(grad_key, cos_table, sin_table, -1.0)
        grad_qkv = jnp.stack([grad_query, grad_key, grad_value], axis=1).reshape(row_count, 3 * D)
        grad_proj = grad_qkv.astype(jnp.bfloat16)
        grad_qkv_b = lax.optimization_barrier(jnp.sum(grad_qkv, axis=0)).reshape(3, D)
        grad_qkv_w = jnp.dot(norm_one.T, grad_proj, preferred_element_type=jnp.float32).reshape(D, 3, D)
        grad_one = jnp.dot(grad_proj, qkv_weight[layer_index].reshape(D, 3 * D).T, preferred_element_type=jnp.float32)
        grad_two = jnp.dot(grad_hidden, up_weight[layer_index].T, preferred_element_type=jnp.float32)
        back_one = jax.vjp(layer_norm, residual, norm_gain[layer_index, 0], norm_shift[layer_index, 0])[1]
        back_two = jax.vjp(layer_norm, residual, norm_gain[layer_index, 1], norm_shift[layer_index, 1])[1]
        through_one, gain_one, shift_one = back_one(grad_one)
        through_two, gain_two, shift_two = back_two(grad_two)
        collected.append((grad_qkv_w, grad_qkv_b, grad_out_w, grad_up_w, grad_up_b, grad_down_w, grad_out_b, jnp.stack([gain_one, gain_two]), jnp.stack([shift_one, shift_two])))
        upstream = upstream + through_one + through_two
    collected = collected[::-1]
    grads = tuple((jnp.stack([entry[member] for entry in collected]) for member in range(9)))
    return (out_row, upstream, grads)

def reference(tokens, doc_ids, qkv_weight, qkv_bias, out_weight, up_weight, up_bias, down_weight, out_bias, norm_gain, norm_shift, cotangent):
    params = (qkv_weight, qkv_bias, out_weight, up_weight, up_bias, down_weight, out_bias, norm_gain, norm_shift)
    token_rows = tokens.reshape(N_DP, TOK_DEV, D)
    cot_rows = cotangent.reshape(N_DP, TOK_DEV, D)

    def scan_rows(carry, item):
        row_tokens, row_docs, row_cot = item
        out_row, grad_row, grads = row_pass(row_tokens, row_docs, row_cot, *params)
        return (jax.tree.map(jnp.add, carry, grads), (out_row, grad_row))
    start_grads = tuple((jnp.zeros(param.shape, jnp.float32) for param in params))
    grads, (out_rows, grad_rows) = lax.scan(scan_rows, start_grads, (token_rows, doc_ids, cot_rows))
    return (out_rows.reshape(TOKENS, D), grad_rows.reshape(TOKENS, D), grads[0], grads[1], grads[2], grads[3], grads[4], grads[5], grads[6], grads[7], grads[8])
```

```python
import math

import jax
import jax.numpy as jnp
from jax import lax
from jax.sharding import Mesh, PartitionSpec as P

HEAD_DIM = 256
ROT_DIMS = 64
HALF = HEAD_DIM // 2

epsilon = 1e-05
rotary_base = 10000.0

f32 = jnp.float32
bf16 = jnp.bfloat16


def dot_nn(a, b):
    return lax.dot_general(a, b, (((1,), (0,)), ((), ())), preferred_element_type=f32)


def dot_nt(a, b):
    return lax.dot_general(a, b, (((1,), (1,)), ((), ())), preferred_element_type=f32)


def dot_tn(a, b):
    return lax.dot_general(a, b, (((0,), (0,)), ((), ())), preferred_element_type=f32)


def swap(value, axis, step=1):
    size = lax.axis_size(axis)
    return lax.ppermute(value, axis, [(i, i ^ step) for i in range(size)])


def relative(value, axis, own):
    size = value.shape[axis]
    if size == 1:
        return value
    if size == 2:
        return jnp.where(own == 0, value, jnp.flip(value, axis))
    return jnp.take(value, jnp.arange(size) ^ own, axis=axis)


def exchange(value, axis):
    return lax.all_to_all(value, axis, 0, 0, tiled=True)


def gelu_exact(values):
    return jax.nn.gelu(values, approximate=False)


def rotate(values, cos_table, sin_table):
    half_width = ROT_DIMS // 2
    first = values[..., :half_width]
    second = values[..., half_width:ROT_DIMS]
    return jnp.concatenate(
        [
            first * cos_table - second * sin_table,
            second * cos_table + first * sin_table,
            values[..., ROT_DIMS:],
        ],
        axis=-1,
    )


def on_device(
    tokens,
    doc_ids,
    qkv_weight,
    qkv_bias,
    out_weight,
    up_weight,
    up_bias,
    down_weight,
    out_bias,
    norm_gain,
    norm_shift,
    cotangent,
):
    row_len, width = tokens.shape
    shard_rows = qkv_weight.shape[1]
    local_cols = qkv_weight.shape[3]
    local_ff = up_weight.shape[2]
    groups = lax.axis_size("col")
    teams = lax.axis_size("team")
    zi, ti = lax.axis_index("col"), lax.axis_index("team")
    yi, ci = lax.axis_index("chip"), lax.axis_index("core")
    pair = zi % 2
    quarter = row_len // 4
    cols = local_cols // groups
    ff = local_ff // groups
    count = groups * row_len

    def features(value):
        lead = value.shape[:-1]
        split = value.reshape(lead + (groups, teams, shard_rows))
        split = jnp.moveaxis(split, -2, len(lead))
        return relative(split, len(lead), ti).reshape(lead + (width,))

    def features_back(value):
        lead = value.shape[:-1]
        split = relative(value.reshape(lead + (teams, groups, shard_rows)), len(lead), ti)
        return jnp.moveaxis(split, len(lead), -2).reshape(lead + (width,))

    def my_quarter(value):
        split = value.reshape(2, 2, quarter, value.shape[-1])
        split = jnp.where(yi == 0, split[0], split[1])
        return jnp.where(ci == 0, split[0], split[1])

    def spread(part):
        part = exchange(jnp.broadcast_to(part[None], (groups,) + part.shape), "col")
        part = part.reshape(count // 4, part.shape[-1])
        part = jnp.concatenate([part, swap(part, "chip")], axis=0)
        return jnp.concatenate([part, swap(part, "core")], axis=0)

    def fold(partial):
        keep, send = partial[: count // 2], partial[count // 2 :]
        partial = keep + swap(send.astype(bf16), "core").astype(f32)
        keep, send = partial[: count // 4], partial[count // 4 :]
        partial = keep + swap(send.astype(bf16), "chip").astype(f32)
        parts = exchange(partial.astype(bf16).reshape(groups, quarter, width), "col")
        return jnp.sum(parts.astype(f32), axis=0)

    def whole_row(part):
        part = jnp.stack([part, swap(part, "chip")])
        part = jnp.stack([part, swap(part, "core")])
        part = relative(relative(part, 0, ci), 1, yi)
        return jnp.swapaxes(part, 0, 1).reshape(row_len, part.shape[-1])

    my_tokens = features(my_quarter(tokens))
    my_cot = features(my_quarter(cotangent))
    gain = features(norm_gain[0])
    shift = features(norm_shift[0])
    residual = spread(my_tokens)
    upstream = spread(my_cot)

    def fetch(block):
        got = exchange(jnp.swapaxes(block, 0, 1), "col").reshape(-1, block.shape[-1])
        return jnp.concatenate([got] + [swap(got, "team", r) for r in range(1, teams)], axis=0)

    qkv_block = jnp.swapaxes(qkv_weight[0].reshape(shard_rows, 3, groups, cols), 1, 2)
    w_qkv = fetch(qkv_block.reshape(shard_rows, groups, 3 * cols))
    w_out = fetch(out_weight[0].reshape(shard_rows, groups, cols))
    w_up = fetch(up_weight[0].reshape(shard_rows, groups, ff))
    w_down = fetch(down_weight[0].reshape(shard_rows, groups, ff))

    docs = exchange(jnp.broadcast_to(doc_ids, (groups, row_len)), "col")
    index = jnp.arange(row_len, dtype=jnp.int32)

    def row_order(value, axis):
        shape = value.shape
        split = value.reshape(shape[:axis] + (2, 2, quarter) + shape[axis + 1 :])
        split = relative(relative(split, axis, yi), axis + 1, ci)
        return jnp.swapaxes(split, axis, axis + 1).reshape(shape)

    docs = row_order(docs, 1)
    index = row_order(index, 0)
    allowed = (docs[:, :, None] == docs[:, None, :]) & (index[None, None, :] <= index[None, :, None])
    position = jnp.sum(allowed.astype(f32), axis=-1) - 1.0
    half_width = ROT_DIMS // 2
    frequency = rotary_base ** (-jnp.arange(half_width).astype(f32) / half_width)
    angles = position[:, :, None] * frequency
    cos_rows, sin_rows = jnp.cos(angles), jnp.sin(angles)

    def to_rows(value):
        split = value.reshape((4, groups, quarter) + value.shape[1:])
        return jnp.swapaxes(split, 0, 1).reshape((groups, row_len) + value.shape[1:])

    def from_rows(value):
        split = value.reshape((groups, 4, quarter) + value.shape[2:])
        return jnp.swapaxes(split, 0, 1).reshape((count,) + value.shape[2:])

    def pair_rows(value):
        split = value.reshape((groups // 2, 2) + value.shape[1:])
        return relative(jnp.swapaxes(split, 0, 1), 0, pair)

    def pair_rows_back(value):
        split = jnp.swapaxes(relative(value, 0, pair), 0, 1)
        return split.reshape((groups,) + value.shape[2:])

    def to_heads(value):
        split = pair_rows(to_rows(value))
        return jnp.stack([split[0], swap(split[1], "col")], axis=-2)

    def from_heads(value):
        mine, other = value[..., 0, :], value[..., 1, :]
        return from_rows(pair_rows_back(jnp.stack([mine, swap(other, "col")])))

    x = residual.astype(f32)
    average = jnp.mean(x, axis=-1, keepdims=True)
    centered = x - average
    inverse = lax.rsqrt(jnp.mean(centered * centered, axis=-1, keepdims=True) + epsilon)
    normal = centered * inverse
    norm_one = (normal * gain[0] + shift[0]).astype(bf16)
    norm_two = (normal * gain[1] + shift[1]).astype(bf16)

    bias_here = lax.dynamic_index_in_dim(qkv_bias[0].reshape(3, groups, cols), zi, 1, False)
    projected = dot_nn(norm_one, w_qkv).reshape(count, 3, cols) + bias_here
    first_half = pair == 0
    cos_mine = jnp.where(first_half, from_rows(cos_rows), 1.0)[:, None]
    sin_mine = jnp.where(first_half, from_rows(sin_rows), 0.0)[:, None]
    turned = jnp.concatenate([rotate(projected[:, :2], cos_mine, sin_mine), projected[:, 2:]], axis=1)
    heads = to_heads(turned.astype(bf16))
    rows_here = groups // 2
    heads = heads.reshape(rows_here, row_len, 3, HEAD_DIM)
    queries, key_rows, value_rows = heads[:, :, 0], heads[:, :, 1], heads[:, :, 2]

    allowed_here = pair_rows(allowed)[0]
    score_scale = 1.0 / math.sqrt(HEAD_DIM)

    def scores_of():
        scores = jnp.einsum("rqe,rke->rqk", queries, key_rows, preferred_element_type=f32)
        return jnp.where(allowed_here, scores * score_scale, -jnp.inf)

    scores = scores_of()
    row_max = jnp.max(scores, axis=-1, keepdims=True)
    log_total = row_max + jnp.log(jnp.sum(jnp.exp(scores - row_max), axis=-1, keepdims=True))
    probs = jnp.exp(scores - log_total)
    soft_weights = probs.astype(bf16)
    context = jnp.einsum("rqk,rke->rqe", soft_weights, value_rows, preferred_element_type=f32)
    context = context.astype(bf16)
    context_cols = from_heads(context.reshape(rows_here, row_len, 1, 2, HALF)).reshape(count, cols)

    up_here = lax.dynamic_index_in_dim(up_bias[0].reshape(groups, ff), zi, 0, False)
    pre_gelu = dot_nn(norm_two, w_up) + up_here
    activated, gelu_back = jax.vjp(gelu_exact, pre_gelu)
    activated = activated.astype(bf16)

    branch = fold(dot_nt(context_cols, w_out) + dot_nt(activated, w_down))
    out_part = my_tokens.astype(f32) + branch + features(out_bias[0])
    output_act = whole_row(features_back(out_part.astype(bf16)))

    grad_context_cols = dot_nn(upstream, w_out).astype(bf16)
    grad_context = to_heads(grad_context_cols[:, None]).reshape(rows_here, row_len, HEAD_DIM)
    grad_pre = gelu_back(dot_nn(upstream, w_down))[0]
    grad_hidden = grad_pre.astype(bf16)

    row_delta = jnp.sum(grad_context.astype(f32) * context.astype(f32), axis=-1, keepdims=True)
    grad_probs = jnp.einsum("rqe,rke->rqk", grad_context, value_rows, preferred_element_type=f32)
    grad_scores = (probs * (grad_probs - row_delta)).astype(bf16)
    grad_query = jnp.einsum("rqk,rke->rqe", grad_scores, key_rows, preferred_element_type=f32)
    grad_key = jnp.einsum("rqk,rqe->rke", grad_scores, queries, preferred_element_type=f32)
    grad_value = jnp.einsum("rqk,rqe->rke", soft_weights, grad_context, preferred_element_type=f32)
    cos_here, sin_here = pair_rows(cos_rows)[0], pair_rows(sin_rows)[0]

    def turn_back(value):
        value = (value * score_scale).reshape(rows_here, row_len, 2, HALF)
        mine = jnp.stack([first_half, ~first_half]).reshape(1, 1, 2, 1)
        cos_both = jnp.where(mine, cos_here[:, :, None], 1.0)
        sin_both = jnp.where(mine, -sin_here[:, :, None], 0.0)
        return rotate(value, cos_both, sin_both)

    grad_qkv = jnp.stack(
        [turn_back(grad_query), turn_back(grad_key), grad_value.reshape(rows_here, row_len, 2, HALF)],
        axis=2,
    )
    bias_sums = jnp.sum(grad_qkv, axis=(0, 1))
    grad_proj = from_heads(grad_qkv.astype(bf16)).reshape(count, 3 * cols)

    grad_one = dot_nt(grad_proj, w_qkv)
    grad_two = dot_nt(grad_hidden, w_up)
    incoming = fold(grad_one * gain[0] + grad_two * gain[1])

    x_mine = my_tokens.astype(f32)
    average = jnp.mean(x_mine, axis=-1, keepdims=True)
    centered = x_mine - average
    inverse = lax.rsqrt(jnp.mean(centered * centered, axis=-1, keepdims=True) + epsilon)
    normal_mine = centered * inverse
    through = inverse * (
        incoming
        - jnp.mean(incoming, axis=-1, keepdims=True)
        - normal_mine * jnp.mean(incoming * normal_mine, axis=-1, keepdims=True)
    )
    grad_part = my_cot.astype(f32) + through
    grad_tokens = whole_row(features_back(grad_part.astype(bf16))).astype(f32)

    def deliver(grad):
        parts = grad.reshape(teams, -1, grad.shape[-1])
        total = parts[0]
        for r in range(1, teams):
            total = total + swap(parts[r].astype(bf16), "team", r).astype(f32)
        got = exchange(total.astype(bf16).reshape(groups, shard_rows, -1), "col")
        return jnp.swapaxes(got.reshape(groups, shard_rows, -1), 0, 1).astype(f32)

    grad_down = deliver(dot_tn(upstream, activated)).reshape(1, shard_rows, local_ff)
    grad_up = deliver(dot_tn(norm_two, grad_hidden)).reshape(1, shard_rows, local_ff)
    grad_out = deliver(dot_tn(upstream, context_cols)).reshape(1, shard_rows, local_cols)
    grad_in = deliver(dot_tn(norm_one, grad_proj)).reshape(shard_rows, groups, 3, cols)
    grad_in = jnp.swapaxes(grad_in, 1, 2).reshape(1, shard_rows, 3, local_cols)

    sums = jnp.stack(
        [
            jnp.sum(grad_one * normal, axis=0),
            jnp.sum(grad_two * normal, axis=0),
            jnp.sum(grad_one, axis=0),
            jnp.sum(grad_two, axis=0),
            jnp.sum(my_cot.astype(f32), axis=0),
        ]
    )
    sums = lax.psum(features_back(sums), ("col", "team", "chip", "core"))
    place = jnp.arange(groups)
    here = jnp.where((place == zi)[None, :, None], bias_sums[:, 0][:, None], 0.0)
    there = jnp.where((place == (zi ^ 1))[None, :, None], bias_sums[:, 1][:, None], 0.0)
    up_sums = jnp.where((place == zi)[:, None], jnp.sum(grad_pre, axis=0)[None], 0.0)
    grad_qkv_bias, grad_up_bias = lax.psum((here + there, up_sums), ("col", "team"))

    return (
        output_act,
        grad_tokens,
        grad_in,
        grad_qkv_bias.reshape(1, 3, local_cols),
        grad_out,
        grad_up,
        grad_up_bias.reshape(1, local_ff),
        grad_down,
        sums[4][None],
        sums[:2][None],
        sums[2:4][None],
    )


def solution(mesh):
    n_dp, n_mp = mesh.shape["dp"], mesh.shape["mp"]
    groups = math.gcd(n_dp, 4)
    grid = Mesh(
        mesh.devices.reshape(groups, n_dp // groups, n_mp // 2, 2),
        ("col", "team", "chip", "core"),
    )
    dp, mp = ("col", "team"), ("chip", "core")
    placed = (
        P(dp, None),
        P(dp, None),
        P(None, dp, None, mp),
        P(None, None, mp),
        P(None, dp, mp),
        P(None, dp, mp),
        P(None, mp),
        P(None, dp, mp),
        P(),
        P(),
        P(),
        P(dp, None),
    )
    return jax.shard_map(
        on_device,
        mesh=grid,
        in_specs=placed,
        out_specs=(
            P(dp, None),
            P(dp, None),
            P(None, dp, None, mp),
            P(None, None, mp),
            P(None, dp, mp),
            P(None, dp, mp),
            P(None, mp),
            P(None, dp, mp),
            P(),
            P(),
            P(),
        ),
        check_vma=False,
    )
```

```python
import math

import jax
import jax.numpy as jnp
from jax import lax
from jax.experimental import pallas as pl
from jax.experimental.pallas import tpu as pltpu
from jax.sharding import Mesh, PartitionSpec as P

HEAD_DIM = 256
ROT_DIMS = 64
HALF = HEAD_DIM // 2

epsilon = 1e-05
rotary_base = 10000.0

f32 = jnp.float32
bf16 = jnp.bfloat16


def dot_nn(a, b):
    return lax.dot_general(a, b, (((1,), (0,)), ((), ())), preferred_element_type=f32)


def dot_nt(a, b):
    return lax.dot_general(a, b, (((1,), (1,)), ((), ())), preferred_element_type=f32)


def dot_tn(a, b):
    return lax.dot_general(a, b, (((0,), (0,)), ((), ())), preferred_element_type=f32)


def swap(value, axis, step=1):
    size = lax.axis_size(axis)
    return lax.ppermute(value, axis, [(i, i ^ step) for i in range(size)])


def relative(value, axis, own):
    size = value.shape[axis]
    if size == 1:
        return value
    if size == 2:
        return jnp.where(own == 0, value, jnp.flip(value, axis))
    return jnp.take(value, jnp.arange(size) ^ own, axis=axis)


def exchange(value, axis):
    return lax.all_to_all(value, axis, 0, 0, tiled=True)


def gelu_exact(values):
    return jax.nn.gelu(values, approximate=False)


def rotate(values, cos_table, sin_table):
    half_width = ROT_DIMS // 2
    first = values[..., :half_width]
    second = values[..., half_width:ROT_DIMS]
    return jnp.concatenate(
        [
            first * cos_table - second * sin_table,
            second * cos_table + first * sin_table,
            values[..., ROT_DIMS:],
        ],
        axis=-1,
    )


def on_device_general(
    tokens,
    doc_ids,
    qkv_weight,
    qkv_bias,
    out_weight,
    up_weight,
    up_bias,
    down_weight,
    out_bias,
    norm_gain,
    norm_shift,
    cotangent,
):
    row_len, width = tokens.shape
    shard_rows = qkv_weight.shape[1]
    local_cols = qkv_weight.shape[3]
    local_ff = up_weight.shape[2]
    groups = lax.axis_size("col")
    teams = lax.axis_size("team")
    zi, ti = lax.axis_index("col"), lax.axis_index("team")
    yi, ci = lax.axis_index("chip"), lax.axis_index("core")
    pair = zi % 2
    quarter = row_len // 4
    cols = local_cols // groups
    ff = local_ff // groups
    count = groups * row_len

    def features(value):
        lead = value.shape[:-1]
        split = value.reshape(lead + (groups, teams, shard_rows))
        split = jnp.moveaxis(split, -2, len(lead))
        return relative(split, len(lead), ti).reshape(lead + (width,))

    def features_back(value):
        lead = value.shape[:-1]
        split = relative(value.reshape(lead + (teams, groups, shard_rows)), len(lead), ti)
        return jnp.moveaxis(split, len(lead), -2).reshape(lead + (width,))

    def my_quarter(value):
        split = value.reshape(2, 2, quarter, value.shape[-1])
        split = jnp.where(yi == 0, split[0], split[1])
        return jnp.where(ci == 0, split[0], split[1])

    def spread(part):
        part = exchange(jnp.broadcast_to(part[None], (groups,) + part.shape), "col")
        part = part.reshape(count // 4, part.shape[-1])
        part = jnp.concatenate([part, swap(part, "chip")], axis=0)
        return jnp.concatenate([part, swap(part, "core")], axis=0)

    def fold(partial):
        keep, send = partial[: count // 2], partial[count // 2 :]
        partial = keep + swap(send.astype(bf16), "core").astype(f32)
        keep, send = partial[: count // 4], partial[count // 4 :]
        partial = keep + swap(send.astype(bf16), "chip").astype(f32)
        parts = exchange(partial.astype(bf16).reshape(groups, quarter, width), "col")
        return jnp.sum(parts.astype(f32), axis=0)

    def whole_row(part):
        part = jnp.stack([part, swap(part, "chip")])
        part = jnp.stack([part, swap(part, "core")])
        part = relative(relative(part, 0, ci), 1, yi)
        return jnp.swapaxes(part, 0, 1).reshape(row_len, part.shape[-1])

    my_tokens = features(my_quarter(tokens))
    my_cot = features(my_quarter(cotangent))
    gain = features(norm_gain[0])
    shift = features(norm_shift[0])
    residual = spread(my_tokens)
    upstream = spread(my_cot)

    def fetch(block):
        got = exchange(jnp.swapaxes(block, 0, 1), "col").reshape(-1, block.shape[-1])
        return jnp.concatenate([got] + [swap(got, "team", r) for r in range(1, teams)], axis=0)

    qkv_block = jnp.swapaxes(qkv_weight[0].reshape(shard_rows, 3, groups, cols), 1, 2)
    w_qkv = fetch(qkv_block.reshape(shard_rows, groups, 3 * cols))
    w_out = fetch(out_weight[0].reshape(shard_rows, groups, cols))
    w_up = fetch(up_weight[0].reshape(shard_rows, groups, ff))
    w_down = fetch(down_weight[0].reshape(shard_rows, groups, ff))

    docs = exchange(jnp.broadcast_to(doc_ids, (groups, row_len)), "col")
    index = jnp.arange(row_len, dtype=jnp.int32)

    def row_order(value, axis):
        shape = value.shape
        split = value.reshape(shape[:axis] + (2, 2, quarter) + shape[axis + 1 :])
        split = relative(relative(split, axis, yi), axis + 1, ci)
        return jnp.swapaxes(split, axis, axis + 1).reshape(shape)

    docs = row_order(docs, 1)
    index = row_order(index, 0)
    allowed = (docs[:, :, None] == docs[:, None, :]) & (index[None, None, :] <= index[None, :, None])
    position = jnp.sum(allowed.astype(f32), axis=-1) - 1.0
    half_width = ROT_DIMS // 2
    frequency = rotary_base ** (-jnp.arange(half_width).astype(f32) / half_width)
    angles = position[:, :, None] * frequency
    cos_rows, sin_rows = jnp.cos(angles), jnp.sin(angles)

    def to_rows(value):
        split = value.reshape((4, groups, quarter) + value.shape[1:])
        return jnp.swapaxes(split, 0, 1).reshape((groups, row_len) + value.shape[1:])

    def from_rows(value):
        split = value.reshape((groups, 4, quarter) + value.shape[2:])
        return jnp.swapaxes(split, 0, 1).reshape((count,) + value.shape[2:])

    def pair_rows(value):
        split = value.reshape((groups // 2, 2) + value.shape[1:])
        return relative(jnp.swapaxes(split, 0, 1), 0, pair)

    def pair_rows_back(value):
        split = jnp.swapaxes(relative(value, 0, pair), 0, 1)
        return split.reshape((groups,) + value.shape[2:])

    def to_heads(value):
        split = pair_rows(to_rows(value))
        return jnp.stack([split[0], swap(split[1], "col")], axis=-2)

    def from_heads(value):
        mine, other = value[..., 0, :], value[..., 1, :]
        return from_rows(pair_rows_back(jnp.stack([mine, swap(other, "col")])))

    x = residual.astype(f32)
    average = jnp.mean(x, axis=-1, keepdims=True)
    centered = x - average
    inverse = lax.rsqrt(jnp.mean(centered * centered, axis=-1, keepdims=True) + epsilon)
    normal = centered * inverse
    norm_one = (normal * gain[0] + shift[0]).astype(bf16)
    norm_two = (normal * gain[1] + shift[1]).astype(bf16)

    bias_here = lax.dynamic_index_in_dim(qkv_bias[0].reshape(3, groups, cols), zi, 1, False)
    projected = dot_nn(norm_one, w_qkv).reshape(count, 3, cols) + bias_here
    first_half = pair == 0
    cos_mine = jnp.where(first_half, from_rows(cos_rows), 1.0)[:, None]
    sin_mine = jnp.where(first_half, from_rows(sin_rows), 0.0)[:, None]
    turned = jnp.concatenate([rotate(projected[:, :2], cos_mine, sin_mine), projected[:, 2:]], axis=1)
    heads = to_heads(turned.astype(bf16))
    rows_here = groups // 2
    heads = heads.reshape(rows_here, row_len, 3, HEAD_DIM)
    queries, key_rows, value_rows = heads[:, :, 0], heads[:, :, 1], heads[:, :, 2]

    allowed_here = pair_rows(allowed)[0]
    score_scale = 1.0 / math.sqrt(HEAD_DIM)

    def scores_of():
        scores = jnp.einsum("rqe,rke->rqk", queries, key_rows, preferred_element_type=f32)
        return jnp.where(allowed_here, scores * score_scale, -jnp.inf)

    scores = scores_of()
    row_max = jnp.max(scores, axis=-1, keepdims=True)
    log_total = row_max + jnp.log(jnp.sum(jnp.exp(scores - row_max), axis=-1, keepdims=True))
    probs = jnp.exp(scores - log_total)
    soft_weights = probs.astype(bf16)
    context = jnp.einsum("rqk,rke->rqe", soft_weights, value_rows, preferred_element_type=f32)
    context = context.astype(bf16)
    context_cols = from_heads(context.reshape(rows_here, row_len, 1, 2, HALF)).reshape(count, cols)

    up_here = lax.dynamic_index_in_dim(up_bias[0].reshape(groups, ff), zi, 0, False)
    pre_gelu = dot_nn(norm_two, w_up) + up_here
    activated, gelu_back = jax.vjp(gelu_exact, pre_gelu)
    activated = activated.astype(bf16)

    branch = fold(dot_nt(context_cols, w_out) + dot_nt(activated, w_down))
    out_part = my_tokens.astype(f32) + branch + features(out_bias[0])
    output_act = whole_row(features_back(out_part.astype(bf16)))

    grad_context_cols = dot_nn(upstream, w_out).astype(bf16)
    grad_context = to_heads(grad_context_cols[:, None]).reshape(rows_here, row_len, HEAD_DIM)
    grad_pre = gelu_back(dot_nn(upstream, w_down))[0]
    grad_hidden = grad_pre.astype(bf16)

    row_delta = jnp.sum(grad_context.astype(f32) * context.astype(f32), axis=-1, keepdims=True)
    grad_probs = jnp.einsum("rqe,rke->rqk", grad_context, value_rows, preferred_element_type=f32)
    grad_scores = (probs * (grad_probs - row_delta)).astype(bf16)
    grad_query = jnp.einsum("rqk,rke->rqe", grad_scores, key_rows, preferred_element_type=f32)
    grad_key = jnp.einsum("rqk,rqe->rke", grad_scores, queries, preferred_element_type=f32)
    grad_value = jnp.einsum("rqk,rqe->rke", soft_weights, grad_context, preferred_element_type=f32)
    cos_here, sin_here = pair_rows(cos_rows)[0], pair_rows(sin_rows)[0]

    def turn_back(value):
        value = (value * score_scale).reshape(rows_here, row_len, 2, HALF)
        mine = jnp.stack([first_half, ~first_half]).reshape(1, 1, 2, 1)
        cos_both = jnp.where(mine, cos_here[:, :, None], 1.0)
        sin_both = jnp.where(mine, -sin_here[:, :, None], 0.0)
        return rotate(value, cos_both, sin_both)

    grad_qkv = jnp.stack(
        [turn_back(grad_query), turn_back(grad_key), grad_value.reshape(rows_here, row_len, 2, HALF)],
        axis=2,
    )
    bias_sums = jnp.sum(grad_qkv, axis=(0, 1))
    grad_proj = from_heads(grad_qkv.astype(bf16)).reshape(count, 3 * cols)

    grad_one = dot_nt(grad_proj, w_qkv)
    grad_two = dot_nt(grad_hidden, w_up)
    incoming = fold(grad_one * gain[0] + grad_two * gain[1])

    x_mine = my_tokens.astype(f32)
    average = jnp.mean(x_mine, axis=-1, keepdims=True)
    centered = x_mine - average
    inverse = lax.rsqrt(jnp.mean(centered * centered, axis=-1, keepdims=True) + epsilon)
    normal_mine = centered * inverse
    through = inverse * (
        incoming
        - jnp.mean(incoming, axis=-1, keepdims=True)
        - normal_mine * jnp.mean(incoming * normal_mine, axis=-1, keepdims=True)
    )
    grad_part = my_cot.astype(f32) + through
    grad_tokens = whole_row(features_back(grad_part.astype(bf16))).astype(f32)

    def deliver(grad):
        parts = grad.reshape(teams, -1, grad.shape[-1])
        total = parts[0]
        for r in range(1, teams):
            total = total + swap(parts[r].astype(bf16), "team", r).astype(f32)
        got = exchange(total.astype(bf16).reshape(groups, shard_rows, -1), "col")
        return jnp.swapaxes(got.reshape(groups, shard_rows, -1), 0, 1).astype(f32)

    grad_down = deliver(dot_tn(upstream, activated)).reshape(1, shard_rows, local_ff)
    grad_up = deliver(dot_tn(norm_two, grad_hidden)).reshape(1, shard_rows, local_ff)
    grad_out = deliver(dot_tn(upstream, context_cols)).reshape(1, shard_rows, local_cols)
    grad_in = deliver(dot_tn(norm_one, grad_proj)).reshape(shard_rows, groups, 3, cols)
    grad_in = jnp.swapaxes(grad_in, 1, 2).reshape(1, shard_rows, 3, local_cols)

    sums = jnp.stack(
        [
            jnp.sum(grad_one * normal, axis=0),
            jnp.sum(grad_two * normal, axis=0),
            jnp.sum(grad_one, axis=0),
            jnp.sum(grad_two, axis=0),
            jnp.sum(my_cot.astype(f32), axis=0),
        ]
    )
    sums = lax.psum(features_back(sums), ("col", "team", "chip", "core"))
    place = jnp.arange(groups)
    here = jnp.where((place == zi)[None, :, None], bias_sums[:, 0][:, None], 0.0)
    there = jnp.where((place == (zi ^ 1))[None, :, None], bias_sums[:, 1][:, None], 0.0)
    up_sums = jnp.where((place == zi)[:, None], jnp.sum(grad_pre, axis=0)[None], 0.0)
    grad_qkv_bias, grad_up_bias = lax.psum((here + there, up_sums), ("col", "team"))

    return (
        output_act,
        grad_tokens,
        grad_in,
        grad_qkv_bias.reshape(1, 3, local_cols),
        grad_out,
        grad_up,
        grad_up_bias.reshape(1, local_ff),
        grad_down,
        sums[4][None],
        sums[:2][None],
        sums[2:4][None],
    )


def lanes(start, size):
    return pl.ds(pl.multiple_of(start, size), size)


def kernel(body, outs, args, grid=(), ins=None, out_specs=None, scratch=(), flops=0):
    nbytes = sum(a.size * a.dtype.itemsize for a in list(args) + list(outs))
    whole = pl.BlockSpec(memory_space=pltpu.VMEM)
    return pl.pallas_call(
        body,
        out_shape=outs,
        grid=grid,
        in_specs=ins if ins is not None else [whole] * len(args),
        out_specs=out_specs if out_specs is not None else [whole] * len(outs),
        scratch_shapes=scratch,
        cost_estimate=pl.CostEstimate(flops=flops, transcendentals=0, bytes_accessed=nbytes),
    )(*args)


def shape(dims, dtype):
    return jax.ShapeDtypeStruct(dims, dtype)


SMEM = pl.BlockSpec(memory_space=pltpu.SMEM)
WHOLE = pl.BlockSpec(memory_space=pltpu.VMEM)


def fixed(dims):
    return pl.BlockSpec(dims, lambda i: (0,) * len(dims))


def tile(dims, turn=0, count=1):
    return pl.BlockSpec(dims, lambda i: ((i + turn) % count if turn else i,) + (0,) * (len(dims) - 1))


def source(where, r, groups):
    return (where[0] ^ (r % groups)) * 2 + (where[1] ^ (r // groups))


def on_device(
    tokens,
    doc_ids,
    qkv_weight,
    qkv_bias,
    out_weight,
    up_weight,
    up_bias,
    down_weight,
    out_bias,
    norm_gain,
    norm_shift,
    cotangent,
):
    row_len, width = tokens.shape
    rows = qkv_weight.shape[1]
    local_cols = qkv_weight.shape[3]
    local_ff = up_weight.shape[2]
    groups = lax.axis_size("col")
    blocks = 2 * groups
    zi, ti = lax.axis_index("col"), lax.axis_index("team")
    yi, ci = lax.axis_index("chip"), lax.axis_index("core")
    cols = local_cols // groups
    ff = local_ff // groups
    quarter = row_len // 4
    count = groups * row_len
    half = count // 2
    side = width // 2
    three = 3 * cols
    where = jnp.stack([zi, ti, yi * 2 + ci, (zi % 2 == 0).astype(jnp.int32)]).astype(jnp.int32)

    def arrange_body(where, tok, cot, gain, shift, bias, gain_o, shift_o, bias_o, *refs):
        mine = pl.ds(pl.multiple_of(where[2] * quarter, quarter), quarter)
        for r in range(blocks):
            src = lanes(source(where, r, groups) * rows, rows)
            gain_o[:, r * rows : (r + 1) * rows] = gain[:, src]
            shift_o[:, r * rows : (r + 1) * rows] = shift[:, src]
            bias_o[:, r * rows : (r + 1) * rows] = bias[:, src]
            tok_r, cot_r = tok[mine, src], cot[mine, src]
            for away in range(groups):
                to = r ^ away
                dst = slice(to * rows, (to + 1) * rows)
                refs[away][:, dst] = tok_r
                refs[groups + away][:, dst] = cot_r

    gain, shift, out_bias_here, *arranged = kernel(
        arrange_body,
        [shape((2, width), f32)] * 2
        + [shape((1, width), f32)]
        + [shape((quarter, width), bf16)] * (2 * groups),
        [where, tokens, cotangent, norm_gain[0], norm_shift[0], out_bias],
        ins=[SMEM] + [WHOLE] * 5,
    )
    token_parts, cot_parts = arranged[:groups], arranged[groups:]
    my_tokens, my_cot = token_parts[0], cot_parts[0]

    def pack_in_body(where, qkv, out, *dst):
        for r in range(groups):
            src = lanes((where[0] ^ r) * cols, cols)
            for p in range(3):
                dst[r][:, p * cols : (p + 1) * cols] = qkv[p, :, src]
            dst[r][:, three:] = out[:, src]

    def pack_ff_body(where, block, *dst):
        for r in range(groups):
            dst[r][...] = block[:, lanes((where[0] ^ r) * ff, ff)]

    qkv_planes = jnp.swapaxes(qkv_weight[0], 0, 1)
    in_send = kernel(
        pack_in_body,
        [shape((rows, three + cols), bf16)] * groups,
        [where, qkv_planes, out_weight[0]],
        ins=[SMEM, WHOLE, WHOLE],
    )
    up_send = kernel(
        pack_ff_body, [shape((rows, ff), bf16)] * groups, [where, up_weight[0]], ins=[SMEM, WHOLE]
    )
    down_send = kernel(
        pack_ff_body, [shape((rows, ff), bf16)] * groups, [where, down_weight[0]], ins=[SMEM, WHOLE]
    )

    def fetch(send):
        got = [send[0]] + [swap(send[r], "col", r) for r in range(1, groups)]
        return got + [swap(block, "team") for block in got]

    def spread(parts):
        got = [parts[0]] + [swap(parts[r], "col", r) for r in range(1, groups)]
        got = jnp.concatenate(got + [swap(block, "chip") for block in got], axis=0)
        return got, swap(got, "core")

    tokens_a, tokens_b = spread(token_parts)
    w_in = fetch(in_send)
    w_up = fetch(up_send)
    up_a, up_b = spread(cot_parts)
    w_down = fetch(down_send)
    upstream = [
        jnp.concatenate([up_a[:, t * side : (t + 1) * side], up_b[:, t * side : (t + 1) * side]])
        for t in range(2)
    ]

    docs = jnp.concatenate([doc_ids] + [swap(doc_ids, "col", r) for r in range(1, groups)], axis=0)
    index = jnp.arange(row_len, dtype=jnp.int32)

    def row_order(value, axis):
        dims = value.shape
        split = value.reshape(dims[:axis] + (2, 2, quarter) + dims[axis + 1 :])
        split = relative(relative(split, axis, yi), axis + 1, ci)
        return jnp.swapaxes(split, axis, axis + 1).reshape(dims)

    docs = row_order(docs, 1)
    index = row_order(index, 0)
    allowed = (docs[:, :, None] == docs[:, None, :]) & (index[None, None, :] <= index[None, :, None])
    position = jnp.sum(allowed.astype(f32), axis=-1) - 1.0
    mask = allowed[0::2].astype(f32)
    half_width = ROT_DIMS // 2
    lane = jnp.arange(HALF)
    frequency = rotary_base ** (-(lane % half_width).astype(f32) / half_width)
    angles = position[:, :, None] * frequency
    cos_table = jnp.where(lane < ROT_DIMS, jnp.cos(angles), 1.0)
    sign = jnp.where(lane < half_width, -1.0, jnp.where(lane < ROT_DIMS, 1.0, 0.0))
    sin_table = jnp.sin(angles) * sign

    def norm_body(a, b, gain, shift, one_l, one_r, two_l, two_r, mean_o, inv_o):
        x = jnp.where(pl.program_id(0) < 2, a[...], b[...]).astype(f32)
        mean = jnp.mean(x, axis=-1, keepdims=True)
        centered = x - mean
        inverse = lax.rsqrt(jnp.mean(centered * centered, axis=-1, keepdims=True) + epsilon)
        normal = centered * inverse
        one = (normal * gain[0:1] + shift[0:1]).astype(bf16)
        two = (normal * gain[1:2] + shift[1:2]).astype(bf16)
        one_l[...] = one[:, :side]
        one_r[...] = one[:, side:]
        two_l[...] = two[:, :side]
        two_r[...] = two[:, side:]
        mean_o[...] = jnp.broadcast_to(mean, mean_o.shape)
        inv_o[...] = jnp.broadcast_to(inverse, inv_o.shape)

    tile_rows = row_len
    steps = count // tile_rows
    first = pl.BlockSpec((tile_rows, width), lambda i: (jnp.minimum(i, 1), 0))
    second = pl.BlockSpec((tile_rows, width), lambda i: (jnp.maximum(i - 2, 0), 0))
    one_l, one_r, two_l, two_r, mean, inverse = kernel(
        norm_body,
        [shape((count, side), bf16)] * 4 + [shape((count, 128), f32)] * 2,
        [tokens_a, tokens_b, gain, shift],
        grid=(steps,),
        ins=[first, second, fixed((2, width)), fixed((2, width))],
        out_specs=[tile((tile_rows, side))] * 4 + [tile((tile_rows, 128))] * 2,
    )

    def times(pair, weights, cut):
        total = None
        for b in range(blocks):
            k = b % groups
            part = dot_nn(pair[b // groups][:, k * rows : (k + 1) * rows], weights[b][:, cut])
            total = part if total is None else total + part
        return total

    def turned(value, cosine, sine):
        at = lax.broadcasted_iota(jnp.int32, value.shape, 1)
        other = jnp.where(
            at < half_width,
            pltpu.roll(value, HALF - half_width, 1),
            pltpu.roll(value, half_width, 1),
        )
        return value * cosine + other * sine

    def qkv_body(where, left, right, cosine, sine, bias, *refs):
        weights, (mine, other) = refs[:blocks], refs[blocks:]
        total = times((left, right), weights, slice(0, three)) + bias[...]
        turn = where[3] == 1
        cosine = jnp.where(turn, cosine[...].reshape(tile_rows, HALF), 1.0)
        sine = jnp.where(turn, sine[...].reshape(tile_rows, HALF), 0.0)
        for p in range(3):
            part = total[:, p * cols : (p + 1) * cols]
            if p < 2:
                part = turned(part, cosine, sine)
            part = part.astype(bf16)
            for r in range(groups):
                dst = mine if r % 2 == 0 else other
                dst[r // 2, :, p * cols : (p + 1) * cols] = part[r * quarter : (r + 1) * quarter]

    qkv_bias_here = lax.dynamic_index_in_dim(qkv_bias[0].reshape(3, groups, cols), zi, 1, False)
    table = pl.BlockSpec((groups, quarter, HALF), lambda i: (0, i, 0))
    here = groups // 2

    def strip(n):
        return pl.BlockSpec((here, quarter, n), lambda i: (0, i, 0))

    heads_mine, heads_other = kernel(
        qkv_body,
        [shape((here, row_len, three), bf16)] * 2,
        [where, one_l, one_r, cos_table, sin_table, qkv_bias_here.reshape(1, three)] + w_in,
        grid=(steps,),
        ins=[SMEM] + [tile((tile_rows, side))] * 2 + [table] * 2 + [fixed((1, three))]
        + [fixed((rows, three + cols))] * blocks,
        out_specs=[strip(three)] * 2,
        flops=2 * count * width * three,
    )
    heads_got = swap(heads_other, "col")

    def grad_context_body(left, right, *refs):
        weights, (mine, other) = refs[:blocks], refs[blocks:]
        part = times((left, right), weights, slice(three, None)).astype(bf16)
        for r in range(groups):
            dst = mine if r % 2 == 0 else other
            dst[r // 2] = part[r * quarter : (r + 1) * quarter]

    gctx_mine, gctx_other = kernel(
        grad_context_body,
        [shape((here, row_len, cols), bf16)] * 2,
        upstream + w_in,
        grid=(steps,),
        ins=[tile((tile_rows, side))] * 2 + [fixed((rows, three + cols))] * blocks,
        out_specs=[strip(cols)] * 2,
        flops=2 * count * width * cols,
    )
    gctx_got = swap(gctx_other, "col")

    def up_body(left, right, bias, *refs):
        weights, (act, slope) = refs[:blocks], refs[blocks:]
        pre = times((left, right), weights, slice(0, ff)) + bias[...]
        below = 0.5 * (1.0 + lax.erf(pre * math.sqrt(0.5)))
        act[...] = (pre * below).astype(bf16)
        slope[...] = below + pre * (jnp.exp(-0.5 * pre * pre) * (1.0 / math.sqrt(2.0 * math.pi)))

    up_bias_here = lax.dynamic_index_in_dim(up_bias[0].reshape(groups, ff), zi, 0, True)
    activated, slope = kernel(
        up_body,
        [shape((count, ff), bf16), shape((count, ff), f32)],
        [two_l, two_r, up_bias_here] + w_up,
        grid=(steps,),
        ins=[tile((tile_rows, side))] * 2 + [fixed((1, ff))] + [fixed((rows, ff))] * blocks,
        out_specs=[tile((tile_rows, ff))] * 2,
        flops=2 * count * width * ff,
    )

    def grad_hidden_body(left, right, slope, *refs):
        weights, (hidden, sums) = refs[:blocks], refs[blocks:]
        grad = times((left, right), weights, slice(0, ff)) * slope[...]
        hidden[...] = grad.astype(bf16)
        part = jnp.sum(grad, axis=0, keepdims=True)

        @pl.when(pl.program_id(0) == 0)
        def _():
            sums[...] = jnp.zeros_like(sums)

        sums[...] += part

    grad_hidden, up_sums = kernel(
        grad_hidden_body,
        [shape((count, ff), bf16), shape((1, ff), f32)],
        upstream + [slope] + w_down,
        grid=(steps,),
        ins=[tile((tile_rows, side))] * 2 + [tile((tile_rows, ff))] + [fixed((rows, ff))] * blocks,
        out_specs=[tile((tile_rows, ff)), fixed((1, ff))],
        flops=2 * count * width * ff,
    )

    score_scale = 1.0 / math.sqrt(HEAD_DIM)

    def attend_body(where, heads_m, heads_o, grad_m, grad_o, mask, cosine, sine, *outs):
        ctx_out, grad_out, sums = outs[:2], outs[2:4], outs[4]
        total = [[None] * 3, [None] * 3]
        for row in range(here):
            part = lambda ref, p: ref[row, :, p * cols : (p + 1) * cols]
            refs = (heads_m, heads_o)
            q, k, v = ([part(ref, p) for ref in refs] for p in range(3))
            g = [grad_m[row], grad_o[row]]
            scores = (dot_nt(q[0], k[0]) + dot_nt(q[1], k[1])) * score_scale
            scores = jnp.where(mask[row] > 0.5, scores, -jnp.inf)
            top = jnp.max(scores, axis=-1, keepdims=True)
            log_total = top + jnp.log(jnp.sum(jnp.exp(scores - top), axis=-1, keepdims=True))
            probs = jnp.exp(scores - log_total)
            soft = probs.astype(bf16)
            ctx = [dot_nn(soft, v[h]).astype(bf16) for h in range(2)]
            delta = sum(
                jnp.sum(g[h].astype(f32) * ctx[h].astype(f32), axis=-1, keepdims=True)
                for h in range(2)
            )
            grad_probs = dot_nt(g[0], v[0]) + dot_nt(g[1], v[1])
            ds = (probs * (grad_probs - delta)).astype(bf16)
            ds_t = ds.T
            soft_t = soft.T
            for h in range(2):
                ctx_out[h][row] = ctx[h]
                turn = (where[3] == 1) if h == 0 else (where[3] == 0)
                cosine_h = jnp.where(turn, cosine[row], 1.0)
                sine_h = jnp.where(turn, -sine[row], 0.0)
                grads = [
                    turned(dot_nn(ds, k[h]) * score_scale, cosine_h, sine_h),
                    turned(dot_nn(ds_t, q[h]) * score_scale, cosine_h, sine_h),
                    dot_nn(soft_t, g[h]),
                ]
                for p in range(3):
                    grad_out[h][row, :, p * cols : (p + 1) * cols] = grads[p].astype(bf16)
                    part_sum = jnp.sum(grads[p], axis=0, keepdims=True)
                    total[h][p] = part_sum if row == 0 else total[h][p] + part_sum
        for h in range(2):
            for p in range(3):
                sums[h : h + 1, p * cols : (p + 1) * cols] = total[h][p]

    ctx_mine, ctx_other, gqkv_mine, gqkv_other, qkv_sums = kernel(
        attend_body,
        [shape((here, row_len, cols), bf16)] * 2
        + [shape((here, row_len, three), bf16)] * 2
        + [shape((2, three), f32)],
        [where, heads_mine, heads_got, gctx_mine, gctx_got, mask, cos_table[0::2], sin_table[0::2]],
        ins=[SMEM] + [WHOLE] * 7,
        flops=2 * here * row_len * row_len * HEAD_DIM * 6,
    )

    def joined(mine, got):
        both = jnp.stack([mine, got], axis=1).reshape(groups, steps, quarter, mine.shape[-1])
        return jnp.swapaxes(both, 0, 1).reshape(count, mine.shape[-1])

    context = joined(ctx_mine, swap(ctx_other, "col"))
    grad_proj = joined(gqkv_mine, swap(gqkv_other, "col"))

    turned_tile = lambda dims: tile(dims, turn=2, count=steps)
    send_spec = pl.BlockSpec((tile_rows, width), lambda i: (jnp.minimum(i, 1), 0))
    keep_spec = pl.BlockSpec((tile_rows, width), lambda i: (jnp.maximum(i - 2, 0), 0))

    def store(send, keep, at, value):
        @pl.when(pl.program_id(0) < 2)
        def _():
            send[:, at] = value.astype(bf16)

        @pl.when(pl.program_id(0) >= 2)
        def _():
            keep[:, at] = value

    def out_body(ctx, act, *refs):
        w_o, w_d, (send, keep) = refs[:blocks], refs[blocks : 2 * blocks], refs[2 * blocks :]
        for b in range(blocks):
            value = dot_nt(ctx[...], w_o[b][:, three:]) + dot_nt(act[...], w_d[b][...])
            store(send, keep, slice(b * rows, (b + 1) * rows), value)

    fold_shapes = [shape((half, width), bf16), shape((half, width), f32)]
    out_send, out_keep = kernel(
        out_body,
        fold_shapes,
        [context, activated] + w_in + w_down,
        grid=(steps,),
        ins=[turned_tile((tile_rows, cols)), turned_tile((tile_rows, ff))]
        + [fixed((rows, three + cols))] * blocks
        + [fixed((rows, ff))] * blocks,
        out_specs=[send_spec, keep_spec],
        flops=2 * count * width * (cols + ff),
    )

    def fold(send, keep):
        got = swap(send, "core")
        quart = half // 2
        got_chip = swap((keep[quart:] + got[quart:].astype(f32)).astype(bf16), "chip")
        total = keep[:quart] + got[:quart].astype(f32) + got_chip.astype(f32)
        parts = total.reshape(groups, quarter, width)
        got_col = [swap(parts[r].astype(bf16), "col", r) for r in range(1, groups)]
        return [parts[0]] + got_col

    def assemble(piece, dtype):
        pieces = [piece, swap(piece, "core"), swap(piece, "chip")]
        across = [((a, b), (1 - a, 1 - b)) for a in range(2) for b in range(2)]
        flat = [(s[0] * 2 + s[1], d[0] * 2 + d[1]) for s, d in across]
        pieces.append(lax.ppermute(piece, ("chip", "core"), flat))

        def body(where, *refs):
            out = refs[-1]
            for q in range(4):
                at = pl.ds(pl.multiple_of((where[2] ^ q) * quarter, quarter), quarter)
                for r in range(blocks):
                    dst = lanes(source(where, r, groups) * rows, rows)
                    out[at, dst] = refs[q][:, r * rows : (r + 1) * rows].astype(dtype)

        return kernel(
            body, [shape((row_len, width), dtype)], [where] + pieces, ins=[SMEM] + [WHOLE] * 4
        )[0]

    def gathered(refs, b):
        total = refs[0][:, b * rows : (b + 1) * rows].astype(f32)
        for r in range(1, groups):
            total = total + refs[r][:, (b ^ r) * rows : ((b ^ r) + 1) * rows].astype(f32)
        return total

    def out_end_body(tok, bias, *refs):
        for b in range(blocks):
            at = slice(b * rows, (b + 1) * rows)
            total = tok[:, at].astype(f32) + bias[:, at] + gathered(refs, b)
            refs[-1][:, at] = total.astype(bf16)

    out_part = kernel(
        out_end_body,
        [shape((quarter, width), bf16)],
        [my_tokens, out_bias_here] + fold(out_send, out_keep),
    )[0]
    output_act = assemble(out_part, bf16)

    def add_stats(stats, at, grad, normal):
        stats[0:1, at] += jnp.sum(grad * normal, axis=0, keepdims=True)
        stats[1:2, at] += jnp.sum(grad, axis=0, keepdims=True)

    def clear(stats):
        @pl.when(pl.program_id(0) == 0)
        def _():
            stats[...] = jnp.zeros_like(stats)

    def normal_of(step, a, b, mean, inverse, at):
        x = jnp.where(step < 2, a[:, at], b[:, at]).astype(f32)
        return (x - mean[:, 0:1]) * inverse[:, 0:1]

    def two_body(hidden, a, b, mean, inverse, gain, *refs):
        weights, (result, stats) = refs[:blocks], refs[blocks:]
        clear(stats)
        for w in range(blocks):
            at = slice(w * rows, (w + 1) * rows)
            grad = dot_nt(hidden[...], weights[w][...])
            add_stats(stats, at, grad, normal_of(pl.program_id(0), a, b, mean, inverse, at))
            result[:, at] = (grad * gain[1:2, at]).astype(bf16)

    from_two, stats_two = kernel(
        two_body,
        [shape((count, width), bf16), shape((2, width), f32)],
        [grad_hidden, tokens_a, tokens_b, mean, inverse, gain] + w_up,
        grid=(steps,),
        ins=[tile((tile_rows, ff)), first, second, tile((tile_rows, 128)), tile((tile_rows, 128))]
        + [fixed((2, width))]
        + [fixed((rows, ff))] * blocks,
        out_specs=[tile((tile_rows, width)), fixed((2, width))],
        flops=2 * count * width * ff,
    )

    def one_body(proj, two, a, b, mean, inverse, gain, *refs):
        weights, (send, keep, stats) = refs[:blocks], refs[blocks:]
        clear(stats)
        for w in range(blocks):
            at = slice(w * rows, (w + 1) * rows)
            grad = dot_nt(proj[...], weights[w][:, :three])
            step = (pl.program_id(0) + 2) % steps
            add_stats(stats, at, grad, normal_of(step, a, b, mean, inverse, at))
            store(send, keep, at, grad * gain[0:1, at] + two[:, at].astype(f32))

    late_first = pl.BlockSpec((tile_rows, width), lambda i: (jnp.maximum(i - 2, 0), 0))
    late_second = pl.BlockSpec((tile_rows, width), lambda i: (jnp.minimum(i, 1), 0))
    in_send_part, in_keep, stats_one = kernel(
        one_body,
        fold_shapes + [shape((2, width), f32)],
        [grad_proj, from_two, tokens_a, tokens_b, mean, inverse, gain] + w_in,
        grid=(steps,),
        ins=[turned_tile((tile_rows, three)), turned_tile((tile_rows, width))]
        + [late_first, late_second]
        + [turned_tile((tile_rows, 128))] * 2
        + [fixed((2, width))]
        + [fixed((rows, three + cols))] * blocks,
        out_specs=[send_spec, keep_spec, fixed((2, width))],
        flops=2 * count * width * three,
    )

    def grad_end_body(tok, cot, *refs):
        x = tok[...].astype(f32)
        mean = jnp.mean(x, axis=-1, keepdims=True)
        centered = x - mean
        inverse = lax.rsqrt(jnp.mean(centered * centered, axis=-1, keepdims=True) + epsilon)
        normal = centered * inverse
        total = jnp.concatenate([gathered(refs, b) for b in range(blocks)], axis=1)
        through = inverse * (
            total
            - jnp.mean(total, axis=-1, keepdims=True)
            - normal * jnp.mean(total * normal, axis=-1, keepdims=True)
        )
        refs[-1][...] = (cot[...].astype(f32) + through).astype(bf16)

    grad_part = kernel(
        grad_end_body,
        [shape((quarter, width), bf16)],
        [my_tokens, my_cot] + fold(in_send_part, in_keep),
    )[0]
    grad_tokens = assemble(grad_part, f32)

    def deliver(left, right):
        got = swap(dot_tn(left[1], right).astype(bf16), "team")
        total = (dot_tn(left[0], right) + got.astype(f32)).astype(bf16)
        parts = [total[r * rows : (r + 1) * rows] for r in range(groups)]
        return [parts[0]] + [swap(parts[r], "col", r) for r in range(1, groups)]

    def place_ff_body(where, *refs):
        for r in range(groups):
            refs[-1][:, lanes((where[0] ^ r) * ff, ff)] = refs[r][...].astype(f32)

    def place_ff(parts):
        return kernel(
            place_ff_body, [shape((rows, local_ff), f32)], [where] + parts, ins=[SMEM] + [WHOLE] * groups
        )[0][None]

    def place_in_body(where, *refs):
        qkv, out = refs[-2:]
        for r in range(groups):
            at = lanes((where[0] ^ r) * cols, cols)
            for p in range(3):
                qkv[p, :, at] = refs[r][:, p * cols : (p + 1) * cols].astype(f32)
            out[:, at] = refs[groups + r][...].astype(f32)

    grad_down = place_ff(deliver(upstream, activated))
    grad_up = place_ff(deliver([two_l, two_r], grad_hidden))
    parts = deliver([one_l, one_r], grad_proj) + deliver(upstream, context)
    grad_qkv_weight, grad_out_weight = kernel(
        place_in_body,
        [shape((3, rows, local_cols), f32), shape((rows, local_cols), f32)],
        [where] + parts,
        ins=[SMEM] + [WHOLE] * (2 * groups),
    )
    grad_qkv_weight = jnp.swapaxes(grad_qkv_weight, 0, 1)[None]

    def collect_body(where, one, two, cot, qkv, up, out):
        out[...] = jnp.zeros_like(out)
        cot_sum = jnp.sum(cot[...].astype(f32), axis=0, keepdims=True)
        for r in range(blocks):
            src = slice(r * rows, (r + 1) * rows)
            dst = lanes(source(where, r, groups) * rows, rows)
            out[0:1, dst] = one[0:1, src]
            out[1:2, dst] = two[0:1, src]
            out[2:3, dst] = one[1:2, src]
            out[3:4, dst] = two[1:2, src]
            out[4:5, dst] = cot_sum[:, src]
        for h in range(2):
            for p in range(3):
                dst = lanes(p * local_cols + (where[0] ^ h) * cols, cols)
                out[5:6, dst] = qkv[h : h + 1, p * cols : (p + 1) * cols]
        out[6:7, lanes(where[0] * ff, ff)] = up[...]

    sums = kernel(
        collect_body,
        [shape((8, max(width, 3 * local_cols, local_ff)), f32)],
        [where, stats_one, stats_two, my_cot, qkv_sums, up_sums],
        ins=[SMEM] + [WHOLE] * 5,
    )[0]
    shared = lax.broadcasted_iota(jnp.int32, sums.shape, 0) < 5
    for axis in ("core", "chip"):
        sums = sums + jnp.where(shared, swap(sums, axis), 0.0)
    for axis, step in (("team", 1), ("col", 1), ("col", 2)):
        sums = sums + swap(sums, axis, step)

    return (
        output_act,
        grad_tokens,
        grad_qkv_weight,
        sums[5, : 3 * local_cols].reshape(1, 3, local_cols),
        grad_out_weight[None],
        grad_up,
        sums[6, :local_ff].reshape(1, local_ff),
        grad_down,
        sums[4, :width][None],
        sums[0:2, :width][None],
        sums[2:4, :width][None],
    )


def solution(mesh):
    n_dp, n_mp = mesh.shape["dp"], mesh.shape["mp"]
    groups = math.gcd(n_dp, 4)
    grid = Mesh(
        mesh.devices.reshape(groups, n_dp // groups, n_mp // 2, 2),
        ("col", "team", "chip", "core"),
    )
    dp, mp = ("col", "team"), ("chip", "core")
    placed = (
        P(dp, None),
        P(dp, None),
        P(None, dp, None, mp),
        P(None, None, mp),
        P(None, dp, mp),
        P(None, dp, mp),
        P(None, mp),
        P(None, dp, mp),
        P(),
        P(),
        P(),
        P(dp, None),
    )
    body = on_device if n_dp // groups == 2 else on_device_general
    return jax.shard_map(
        body,
        mesh=grid,
        in_specs=placed,
        out_specs=(
            P(dp, None),
            P(dp, None),
            P(None, dp, None, mp),
            P(None, None, mp),
            P(None, dp, mp),
            P(None, dp, mp),
            P(None, mp),
            P(None, dp, mp),
            P(),
            P(),
            P(),
        ),
        check_vma=False,
    )
```
